32 devices in a mesh: groups: 2 (over y), wide: 4 (over z), heads: 4 (over x, core).
Axes of the slice: x: 2, y: 2, z: 4, core: 2. Of those that a mesh axis runs over, the one named last changes fastest.
Arguments:
- video_hidden: bfloat16 [2048, 4096], P(('groups', 'wide'), 'heads'), parts along dimension 0, may hold values from -6 to 6
- audio_hidden: bfloat16 [512, 2048], P(('groups', 'wide'), 'heads'), parts along dimension 0, may hold values from -6 to 6
- video_query: bfloat16 [2048, 2048], P(('groups', 'wide'), 'heads'), parts along dimension 0, may hold values from -8 to 8
- video_key: bfloat16 [2048, 2048], P(('groups', 'wide'), 'heads'), parts along dimension 0, may hold values from -8 to 8
- video_value: bfloat16 [2048, 2048], P(('groups', 'wide'), 'heads'), parts along dimension 0, may hold values from -6 to 6
- audio_query: bfloat16 [512, 1024], P(('groups', 'wide'), 'heads'), parts along dimension 0, may hold values from -8 to 8
- audio_key: bfloat16 [512, 1024], P(('groups', 'wide'), 'heads'), parts along dimension 0, may hold values from -8 to 8
- audio_value: bfloat16 [512, 1024], P(('groups', 'wide'), 'heads'), parts along dimension 0, may hold values from -6 to 6
- cross_video_query: bfloat16 [2048, 1024], P(('groups', 'wide'), 'heads'), parts along dimension 0, may hold values from -8 to 8
- cross_audio_key: bfloat16 [512, 1024], P(('groups', 'wide'), 'heads'), parts along dimension 0, may hold values from -8 to 8
- cross_audio_value: bfloat16 [512, 1024], P(('groups', 'wide'), 'heads'), parts along dimension 0, may hold values from -6 to 6
- cross_audio_query: bfloat16 [512, 1024], P(('groups', 'wide'), 'heads'), parts along dimension 0, may hold values from -8 to 8
- cross_video_key: bfloat16 [2048, 1024], P(('groups', 'wide'), 'heads'), parts along dimension 0, may hold values from -8 to 8
- cross_video_value: bfloat16 [2048, 1024], P(('groups', 'wide'), 'heads'), parts along dimension 0, may hold values from -6 to 6
- video_self_out: bfloat16 [2048, 4096], P('heads', 'wide'), may hold values from -0.125 to 0.125
- video_cross_out: bfloat16 [1024, 4096], P('heads', 'wide'), may hold values from -0.1875 to 0.1875
- audio_self_out: bfloat16 [1024, 2048], P('heads', 'wide'), may hold values from -0.1875 to 0.1875
- audio_cross_out: bfloat16 [1024, 2048], P('heads', 'wide'), may hold values from -0.1875 to 0.1875
- intersection: int32 [8, 5], P('groups'), parts along dimension 0, may hold values from 0 to 1, as said below
Outputs:
- video_out: bfloat16 [2048, 4096], P(('groups', 'wide'), 'heads'), parts along dimension 0
- audio_out: bfloat16 [512, 2048], P(('groups', 'wide'), 'heads'), parts along dimension 0
The draws below stay inside these ranges and needn't reach their ends.
There are 2 independent parts, one for each index of `groups`. The reference program is written for one: setup_inputs(seed, part) draws one part's arguments, and reference() takes and returns one part's arrays. A program takes and returns all parts, laid end to end along the dimension named above; an argument that names none is the same for every part. Nothing has to cross between parts.
Inputs may be any that keep to these rules, and one draw needn't show every extreme that they name: `intersection`: column 2 is 1 in every row; entries that would pair a block with one outside the clip are ignored.
All inputs are finite; a program needn't handle non-finite values.
Results may differ from the reference program's by a relative error of at most 0.012.
Values may be sent and summed in bfloat16 or wider, within the bound.
A program may use at most 64 MiB of HBM per device.

```python
import math
import jax
import jax.numpy as jnp
from jax import lax

DV = 4096
DA = 2048
HDV = 128
HDA = 64
HEADS = 16
REACH = 2
TV_DEV = 256
TA_DEV = 64
SPAN = 5
BLOCKS = 4
NV = 1024
NA = 256
N_HEADS = 4


def attention_pair(base_key, query_count, key_count, head_size):
    split_keys = jax.random.split(base_key, 2)
    queries = jnp.clip(3.0 * jax.random.normal(split_keys[0], (query_count, HEADS * head_size), jnp.float32), -8.0, 8.0)
    key_rows = jnp.clip(jax.random.normal(split_keys[1], (key_count, HEADS * head_size), jnp.float32), -4.0, 4.0)
    return (queries, key_rows)


def draw_video_query(key, part):
    return attention_pair(jax.random.fold_in(key, 11), NV, NV, HDV)[0].astype(jnp.bfloat16)


def draw_video_key(key, part):
    return attention_pair(jax.random.fold_in(key, 11), NV, NV, HDV)[1].astype(jnp.bfloat16)


def draw_audio_query(key, part):
    return attention_pair(jax.random.fold_in(key, 12), NA, NA, HDA)[0].astype(jnp.bfloat16)


def draw_audio_key(key, part):
    return attention_pair(jax.random.fold_in(key, 12), NA, NA, HDA)[1].astype(jnp.bfloat16)


def draw_cross_video_query(key, part):
    return attention_pair(jax.random.fold_in(key, 13), NV, NA, HDA)[0].astype(jnp.bfloat16)


def draw_cross_audio_key(key, part):
    return attention_pair(jax.random.fold_in(key, 13), NV, NA, HDA)[1].astype(jnp.bfloat16)


def draw_cross_audio_query(key, part):
    return attention_pair(jax.random.fold_in(key, 14), NA, NV, HDA)[0].astype(jnp.bfloat16)


def draw_cross_video_key(key, part):
    return attention_pair(jax.random.fold_in(key, 14), NA, NV, HDA)[1].astype(jnp.bfloat16)


def draw_intersection(key, part):
    level_key, rolled_key = jax.random.split(jax.random.fold_in(key, 15))
    levels = jax.random.randint(level_key, (BLOCKS, 1), 1, 5)
    rolled = jax.random.randint(rolled_key, (BLOCKS, SPAN), 0, 5)
    intersection_table = (rolled < levels).astype(jnp.int32)
    column = jnp.arange(SPAN, dtype=jnp.int32)
    return jnp.where(column[None, :] == REACH, 1, intersection_table).astype(jnp.int32)


def steps_of(stream_key, extent, cuts, least, top_value):
    gain = 1.0
    for dim, shards_of in cuts:
        draws = jax.random.uniform(jax.random.fold_in(jax.random.fold_in(stream_key, 6), dim), (shards_of,), jnp.float32, least / len(cuts), top_value / len(cuts))
        gain = gain * jnp.repeat(jnp.exp(draws), extent[dim] // shards_of).reshape((-1,) + (1,) * (len(extent) - 1 - dim))
    return gain


def noise(key, shape, spread, bound, cuts=(), held_as=jnp.bfloat16):
    values = spread * jax.random.normal(key, shape, jnp.float32)
    if cuts:
        values = values * steps_of(key, shape, cuts, -0.22, 0.18)
    return jnp.clip(values, -bound, bound).astype(held_as)


def setup_inputs(seed: int = 0, part: int = 0) -> dict:
    splits = jax.random.split(jax.random.key(seed), 20)
    part_keys = jax.random.split(jax.random.fold_in(splits[19], part), 20)
    return {
        "video_hidden": noise(part_keys[0], (NV, DV), 1.0, 6.0, ((0, 4), (1, 4))),
        "audio_hidden": noise(part_keys[1], (NA, DA), 1.0, 6.0, ((0, 4), (1, 4))),
        "video_query": draw_video_query(jax.random.fold_in(jax.random.fold_in(splits[19], part), 71), part),
        "video_key": draw_video_key(jax.random.fold_in(jax.random.fold_in(splits[19], part), 71), part),
        "video_value": noise(part_keys[4], (NV, HEADS * HDV), 1.0, 6.0, ((0, 4), (1, 4))),
        "audio_query": draw_audio_query(jax.random.fold_in(jax.random.fold_in(splits[19], part), 71), part),
        "audio_key": draw_audio_key(jax.random.fold_in(jax.random.fold_in(splits[19], part), 71), part),
        "audio_value": noise(part_keys[7], (NA, HEADS * HDA), 1.0, 6.0, ((0, 4), (1, 4))),
        "cross_video_query": draw_cross_video_query(jax.random.fold_in(jax.random.fold_in(splits[19], part), 71), part),
        "cross_audio_key": draw_cross_audio_key(jax.random.fold_in(jax.random.fold_in(splits[19], part), 71), part),
        "cross_audio_value": noise(part_keys[10], (NA, HEADS * HDA), 1.0, 6.0, ((0, 4), (1, 4))),
        "cross_audio_query": draw_cross_audio_query(jax.random.fold_in(jax.random.fold_in(splits[19], part), 71), part),
        "cross_video_key": draw_cross_video_key(jax.random.fold_in(jax.random.fold_in(splits[19], part), 71), part),
        "cross_video_value": noise(part_keys[13], (NV, HEADS * HDA), 1.0, 6.0, ((0, 4), (1, 4))),
        "video_self_out": noise(splits[14], (HEADS * HDV, DV), (HEADS * HDV) ** -0.5, 0.125, ((0, 4), (1, 4))),
        "video_cross_out": noise(splits[15], (HEADS * HDA, DV), (HEADS * HDA) ** -0.5, 0.1875, ((0, 4), (1, 4))),
        "audio_self_out": noise(splits[16], (HEADS * HDA, DA), (HEADS * HDA) ** -0.5, 0.1875, ((0, 4), (1, 4))),
        "audio_cross_out": noise(splits[17], (HEADS * HDA, DA), (HEADS * HDA) ** -0.5, 0.1875, ((0, 4), (1, 4))),
        "intersection": draw_intersection(jax.random.fold_in(jax.random.fold_in(splits[19], part), 71), part),
    }


def attend(queries, key_rows, value_rows, head_size, allowed):
    row_count = queries.shape[0]
    query_heads = queries.reshape(row_count, HEADS, head_size).transpose(1, 0, 2)
    key_heads = key_rows.reshape(key_rows.shape[0], HEADS, head_size).transpose(1, 0, 2)
    value_heads = value_rows.reshape(value_rows.shape[0], HEADS, head_size).transpose(1, 0, 2)

    def one_head(operands):
        query_one, key_one, value_one = operands
        scores = jnp.dot(query_one, key_one.T, preferred_element_type=jnp.float32) * (1.0 / math.sqrt(head_size))
        if allowed is not None:
            scores = jnp.where(allowed, scores, -1e+30)
        maximum = lax.optimization_barrier(jnp.max(scores, axis=1, keepdims=True))
        weights = jnp.exp(scores - maximum)
        if allowed is not None:
            weights = jnp.where(allowed, weights, 0.0)
        totals = lax.optimization_barrier(jnp.sum(weights, axis=1, keepdims=True))
        mixed = jnp.dot(weights.astype(jnp.bfloat16), value_one, preferred_element_type=jnp.float32)
        return (mixed / totals).astype(jnp.bfloat16)
    result = lax.map(one_head, (query_heads, key_heads, value_heads))
    return result.transpose(1, 0, 2).reshape(row_count, HEADS * head_size)

def cross_mask(intersection):
    video_blocks = jnp.arange(NV, dtype=jnp.int32) // TV_DEV
    audio_blocks = jnp.arange(NA, dtype=jnp.int32) // TA_DEV
    offsets = audio_blocks[None, :] - video_blocks[:, None] + REACH
    inside = (offsets >= 0) & (offsets < SPAN)
    picked = intersection[video_blocks[:, None], jnp.clip(offsets, 0, SPAN - 1)]
    return inside & (picked > 0)

def project(self_part, cross_part, self_weight, cross_weight, self_size, cross_size, hidden):
    per_group = HEADS // N_HEADS
    total = hidden.astype(jnp.float32)
    for head_group in range(N_HEADS):
        self_cols = self_part[:, head_group * per_group * self_size:(head_group + 1) * per_group * self_size]
        cross_cols = cross_part[:, head_group * per_group * cross_size:(head_group + 1) * per_group * cross_size]
        self_rows = self_weight[head_group * per_group * self_size:(head_group + 1) * per_group * self_size]
        cross_rows = cross_weight[head_group * per_group * cross_size:(head_group + 1) * per_group * cross_size]
        partial_value = jnp.dot(self_cols, self_rows, preferred_element_type=jnp.float32) + jnp.dot(cross_cols, cross_rows, preferred_element_type=jnp.float32)
        total = total + lax.optimization_barrier(partial_value.astype(jnp.bfloat16)).astype(jnp.float32)
    return total.astype(jnp.bfloat16)

def reference(video_hidden, audio_hidden, video_query, video_key, video_value, audio_query, audio_key, audio_value, cross_video_query, cross_audio_key, cross_audio_value, cross_audio_query, cross_video_key, cross_video_value, video_self_out, video_cross_out, audio_self_out, audio_cross_out, intersection):
    video_self = attend(video_query, video_key, video_value, HDV, None)
    audio_self = attend(audio_query, audio_key, audio_value, HDA, None)
    allowed = cross_mask(intersection)
    video_cross = attend(cross_video_query, cross_audio_key, cross_audio_value, HDA, allowed)
    audio_cross = attend(cross_audio_query, cross_video_key, cross_video_value, HDA, allowed.T)
    video_out = project(video_self, video_cross, video_self_out, video_cross_out, HDV, HDA, video_hidden)
    audio_out = project(audio_self, audio_cross, audio_self_out, audio_cross_out, HDA, HDA, audio_hidden)
    return (video_out, audio_out)
```

```python
import functools
import math

import jax
import jax.numpy as jnp
from jax import lax
from jax.experimental import pallas as pl
from jax.experimental.pallas import tpu as pltpu
from jax.sharding import PartitionSpec as P

HDV = 128
HDA = 64
REACH = 2


def passed_along(value, axis, by):
    length = lax.axis_size(axis)
    pairs = [(i, i + by) for i in range(length) if 0 <= i + by < length]
    return lax.ppermute(value, axis, pairs)


def empty_state(row_count, head_count, head_size):
    return (
        jnp.full((head_count, row_count), -1e30, jnp.float32),
        jnp.zeros((head_count, row_count), jnp.float32),
        jnp.zeros((head_count, row_count, head_size), jnp.float32),
    )


def absorb(state, queries, key_rows, value_rows, head_size, allowed):
    maxima, totals, running = state
    head_count = queries.shape[1] // head_size
    query_heads = queries.reshape(queries.shape[0], head_count, head_size)
    key_heads = key_rows.reshape(key_rows.shape[0], head_count, head_size)
    value_heads = value_rows.reshape(value_rows.shape[0], head_count, head_size)
    scores = jnp.einsum(
        "qhd,khd->hqk", query_heads, key_heads, preferred_element_type=jnp.float32
    ) * (1.0 / math.sqrt(head_size))
    if allowed is not None:
        scores = jnp.where(allowed[None, None, :], scores, -1e30)
    new_peak = jnp.maximum(maxima, jnp.max(scores, axis=2))
    weights = jnp.exp(scores - new_peak[:, :, None])
    if allowed is not None:
        weights = jnp.where(allowed[None, None, :], weights, 0.0)
    rescale = jnp.exp(maxima - new_peak)
    totals = totals * rescale + jnp.sum(weights, axis=2)
    running = running * rescale[:, :, None] + jnp.einsum(
        "hqk,khd->hqd",
        weights.astype(jnp.bfloat16),
        value_heads,
        preferred_element_type=jnp.float32,
    )
    return (new_peak, totals, running)


def finish(state, head_size):
    maxima, totals, running = state
    result = running / totals[:, :, None]
    return (
        result.transpose(1, 0, 2)
        .reshape(result.shape[1], result.shape[0] * head_size)
        .astype(jnp.bfloat16)
    )


def permitted(key_blocks, position, table_row, wide_count):
    offsets = key_blocks - position + REACH
    matches = (offsets[:, None] == jnp.arange(2 * REACH + 1, dtype=jnp.int32)[None, :]) & (
        table_row[None, :] > 0
    )
    inside = (key_blocks >= 0) & (key_blocks < wide_count)
    return jnp.any(matches, axis=1) & inside


def general_shards(
    video_hidden,
    audio_hidden,
    video_query,
    video_key,
    video_value,
    audio_query,
    audio_key,
    audio_value,
    cross_video_query,
    cross_audio_key,
    cross_audio_value,
    cross_audio_query,
    cross_video_key,
    cross_video_value,
    video_self_out,
    video_cross_out,
    audio_self_out,
    audio_cross_out,
    intersection,
):
    position = lax.axis_index("wide")
    wide_count = lax.axis_size("wide")
    video_count = video_query.shape[0]
    audio_count = audio_query.shape[0]
    head_count = video_query.shape[1] // HDV
    video_start = empty_state(video_count, head_count, HDV)
    audio_start = empty_state(audio_count, head_count, HDA)
    carried = (video_start, audio_start)
    portion = (
        lax.all_gather(video_key, "wide", axis=0, tiled=True),
        lax.all_gather(video_value, "wide", axis=0, tiled=True),
        lax.all_gather(audio_key, "wide", axis=0, tiled=True),
        lax.all_gather(audio_value, "wide", axis=0, tiled=True),
    )
    video_state = absorb(carried[0], video_query, portion[0], portion[1], HDV, None)
    audio_state = absorb(carried[1], audio_query, portion[2], portion[3], HDA, None)
    table_row = lax.dynamic_slice_in_dim(intersection, position, 1, 0)[0]
    padded_table = jnp.pad(intersection, ((REACH, REACH), (0, 0)))
    flag_row = jnp.diagonal(
        jnp.fliplr(lax.dynamic_slice_in_dim(padded_table, position, 2 * REACH + 1, 0))
    )
    stacked = jnp.concatenate(
        [cross_audio_key, cross_audio_value, cross_video_key, cross_video_value], 0
    )

    def take_cross(carried, portion, block):
        audio_keys = portion[:audio_count]
        audio_values = portion[audio_count : 2 * audio_count]
        video_keys = portion[2 * audio_count : 2 * audio_count + video_count]
        video_values = portion[2 * audio_count + video_count :]
        audio_blocks = jnp.full((audio_count,), block, jnp.int32)
        video_blocks = jnp.full((video_count,), block, jnp.int32)
        return (
            absorb(
                carried[0],
                cross_video_query,
                audio_keys,
                audio_values,
                HDA,
                permitted(audio_blocks, position, table_row, wide_count),
            ),
            absorb(
                carried[1],
                cross_audio_query,
                video_keys,
                video_values,
                HDA,
                permitted(video_blocks, position, flag_row, wide_count),
            ),
        )

    cross_start = (
        empty_state(video_count, head_count, HDA),
        empty_state(audio_count, head_count, HDA),
    )
    carried = take_cross(cross_start, stacked, position)
    for offset in range(-REACH, REACH + 1):
        if offset != 0:
            nearby = passed_along(stacked, "wide", -offset)
            carried = take_cross(carried, nearby, position + offset)
    to_video, to_audio = carried
    video_joined = jnp.concatenate([finish(video_state, HDV), finish(to_video, HDA)], 1)
    audio_joined = jnp.concatenate([finish(audio_state, HDA), finish(to_audio, HDA)], 1)
    video_weights = jnp.concatenate([video_self_out, video_cross_out], 0)
    audio_weights = jnp.concatenate([audio_self_out, audio_cross_out], 0)
    video_terms = jnp.dot(
        video_joined,
        lax.all_gather(video_weights, "wide", axis=1, tiled=True),
        preferred_element_type=jnp.float32,
    )
    audio_terms = jnp.dot(
        audio_joined,
        lax.all_gather(audio_weights, "wide", axis=1, tiled=True),
        preferred_element_type=jnp.float32,
    )
    video_sum, audio_sum = (
        lax.psum_scatter(
            video_terms.astype(jnp.bfloat16), "heads", scatter_dimension=1, tiled=True
        ).astype(jnp.float32),
        lax.psum_scatter(
            audio_terms.astype(jnp.bfloat16), "heads", scatter_dimension=1, tiled=True
        ).astype(jnp.float32),
    )
    video_out = (video_hidden.astype(jnp.float32) + video_sum).astype(jnp.bfloat16)
    audio_out = (audio_hidden.astype(jnp.float32) + audio_sum).astype(jnp.bfloat16)
    return (video_out, audio_out)


NT = (((1,), (1,)), ((), ()))
MESH = pl.DeviceIdType.MESH


def pack_kernel(n, cvq, cvk, cvv, aq, ak, av, caq, cak, cav, aso, aco, pack, wa):
    rows = cvq.shape[0]
    half = rows // 2
    few = aq.shape[0]
    for j in range(n):
        cols = slice(j * HDA, (j + 1) * HDA)
        pack[j, :rows, :] = jnp.concatenate([cvq[:, cols], cvk[:, cols]], 1)
        pack[j, rows : rows + half, :] = jnp.concatenate([cvv[:half, cols], cvv[half:, cols]], 1)
        at = rows + half
        for left, right in ((aq, ak), (av, caq), (cak, cav)):
            pack[j, at : at + few, :] = jnp.concatenate([left[:, cols], right[:, cols]], 1)
            at += few
        wa[2 * j * HDA : (2 * j + 1) * HDA, :] = aso[cols, :]
        wa[(2 * j + 1) * HDA : (2 * j + 2) * HDA, :] = aco[cols, :]


def attend(queries, keys, values, head_size, bias):
    scores = lax.dot_general(queries, keys, NT, preferred_element_type=jnp.float32)
    scores = scores * (1.0 / math.sqrt(head_size))
    if bias is not None:
        scores = scores + bias
    weights = jnp.exp(scores - jnp.max(scores, axis=1, keepdims=True))
    totals = jnp.sum(weights, axis=1, keepdims=True)
    mixed = jnp.dot(weights.astype(jnp.bfloat16), values, preferred_element_type=jnp.float32)
    return (mixed / totals).astype(jnp.bfloat16)


def fused_kernel(
    n, chunks,
    vq, vk, vv, pack, ws, wc, wa, bias_v, bias_a,
    out_v, out_a,
    q_all, k_all, v_all, p_all, ws_all, wc_all, wa_all,
    o_self, o_rest, r_self, r_rest, sum_v, sum_a,
    a_send, a_recv, w_send, w_recv, f_send, f_recv, b_send, b_recv, d_send, d_recv, local,
):
    w = lax.axis_index("wide")
    h = lax.axis_index("heads")
    rows = vq.shape[0]
    half = rows // 2
    few = out_a.shape[0]

    def place(dw, dh):
        return {"wide": lax.rem(w + dw, n), "heads": lax.rem(h + dh, n)}

    def remote(source, target, send, recv, device):
        return pltpu.make_async_remote_copy(
            src_ref=source, dst_ref=target, send_sem=send, recv_sem=recv,
            device_id=device, device_id_type=MESH,
        )

    others = [(dw, dh) for dw in range(n) for dh in range(n) if dw or dh]
    barrier = pltpu.get_barrier_semaphore()
    for dw, dh in others:
        pl.semaphore_signal(barrier, inc=1, device_id=place(dw, dh), device_id_type=MESH)

    def head_cols(ref, who):
        return ref.at[:, pl.ds(pl.multiple_of(who * HDV, HDV), HDV)]

    own = [pltpu.make_async_copy(pack.at[w], p_all.at[w], local.at[0])]
    for i, (source, target) in enumerate(((vk, k_all), (vv, v_all), (vq, q_all))):
        own.append(pltpu.make_async_copy(head_cols(source, w), target.at[w], local.at[1 + i]))
    for i, (source, target) in enumerate(((ws, ws_all), (wc, wc_all), (wa, wa_all))):
        own.append(pltpu.make_async_copy(source, target.at[h], local.at[4 + i]))
    for copy in own:
        copy.start()
    pl.semaphore_wait(barrier, len(others))

    a_copies = {}
    for i, (source, target) in enumerate(((pack, p_all), (vk, k_all), (vv, v_all), (vq, q_all))):
        for d in range(1, n):
            who = lax.rem(w + d, n)
            piece = source.at[who] if i == 0 else head_cols(source, who)
            copy = remote(piece, target.at[w], a_send.at[i, d], a_recv.at[i, d], place(d, 0))
            copy.start()
            a_copies[i, d] = copy

    pairs = ((ws, ws_all), (wc, wc_all), (wa, wa_all))
    partner = {"wide": w, "heads": h + 1 - 2 * lax.rem(h, 2)}
    w_copies, f_copies = [], []
    for i, (source, target) in enumerate(pairs):
        for k in range(1, n // 2):
            copy = remote(source, target.at[h], w_send.at[i, k], w_recv.at[i, k], place(0, 2 * k))
            copy.start()
            w_copies.append(copy)
        copy = remote(source, target.at[h], f_send.at[i, 0], f_recv.at[i, 0], partner)
        copy.start()
        f_copies.append(copy)

    own[0].wait()
    for d in range(1, n):
        a_copies[0, d].wait_recv()
    at = rows + half

    def part(j, start, right):
        return p_all[j, start : start + few, HDA:] if right else p_all[j, start : start + few, :HDA]

    def whole(start, right):
        return jnp.concatenate([part(j, start, right) for j in range(n)], 0)

    aq, ak = whole(at, False), whole(at, True)
    av, caq = whole(at + few, False), whole(at + few, True)
    cak, cav = whole(at + 2 * few, False), whole(at + 2 * few, True)
    cvk = jnp.concatenate([p_all[j, :rows, HDA:] for j in range(n)], 0)
    cvv = jnp.concatenate(
        [p_all[j, rows:at, cols] for j in range(n) for cols in (slice(0, HDA), slice(HDA, 2 * HDA))], 0
    )
    wide_bias = jnp.concatenate(
        [jnp.broadcast_to(bias_a[j : j + 1, :], (few, bias_a.shape[1])) for j in range(n)], 0
    )
    audio = jnp.concatenate(
        [attend(aq, ak, av, HDA, None), attend(caq, cvk, cvv, HDA, wide_bias)], 1
    )
    for j in range(n):
        o_rest[j, half:, :] = audio[j * few : (j + 1) * few, :]
        mixed = attend(p_all[j, :rows, :HDA], cak, cav, HDA, bias_v[j : j + 1, :])
        o_rest[j, :half, :] = jnp.concatenate([mixed[:half], mixed[half:]], 1)

    mine = h * n + w
    b_copies = {}

    def spread(kind, buffer, landing, dh):
        block = lax.rem(h + dh, n)
        for dw in range(n):
            if dw or dh:
                slot = dw * n + dh
                copy = remote(
                    buffer.at[block], landing.at[mine],
                    b_send.at[kind, slot], b_recv.at[kind, slot], place(dw, dh),
                )
                copy.start()
                b_copies[kind, slot] = copy

    for dh in list(range(1, n)) + [0]:
        spread(0, o_rest, r_rest, dh)
    r_rest[pl.ds(mine, 1)] = o_rest[pl.ds(h, 1)]

    for i in range(1, 4):
        own[i].wait()
        for d in range(1, n):
            a_copies[i, d].wait_recv()
    keys = k_all[...].reshape(n * rows, HDV)
    values = v_all[...].reshape(n * rows, HDV)
    for dh in list(range(1, n)) + [0]:
        block = lax.rem(h + dh, n)
        o_self[pl.ds(block, 1)] = attend(
            q_all[pl.ds(block, 1)].reshape(rows, HDV), keys, values, HDV, None
        )[None]
        spread(1, o_self, r_self, dh)
    r_self[pl.ds(mine, 1)] = o_self[pl.ds(h, 1)]

    for copy in w_copies:
        copy.wait_recv()
    for i, (source, target) in enumerate(pairs):
        for k in range(1, n // 2):
            slot = lax.rem(h + n - 2 * k, n)
            copy = remote(target.at[slot], target.at[slot], f_send.at[i, k], f_recv.at[i, k], partner)
            copy.start()
            f_copies.append(copy)

    for copy in own[4:]:
        copy.wait()
    for copy in b_copies.values():
        copy.wait_recv()
    for copy in f_copies:
        copy.wait_recv()

    heads = n * n
    joined = jnp.concatenate([r_self[s] for s in range(heads)], 1)
    crossed = jnp.concatenate(
        [
            jnp.concatenate([r_rest[s, :half, :HDA] for s in range(heads)], 1),
            jnp.concatenate([r_rest[s, :half, HDA:] for s in range(heads)], 1),
        ],
        0,
    )
    audio_joined = jnp.concatenate([r_rest[s, half:, :] for s in range(heads)], 1)
    home = {"wide": h, "heads": w}
    sums = jnp.dot(
        audio_joined, wa_all[...].reshape(-1, wa.shape[1]), preferred_element_type=jnp.float32
    )
    sum_a[...] = sums.astype(jnp.bfloat16)
    width = ws.shape[1] // chunks
    pieces = [(sum_a, out_a)]
    last = []

    def deliver(i, source, target):
        away = remote(source, target, d_send.at[i], d_recv.at[i], home)
        here = pltpu.make_async_copy(source, target, local.at[7 + i])
        last.append((away, here))

        @pl.when(w != h)
        def _():
            away.start()

        @pl.when(w == h)
        def _():
            here.start()

    deliver(0, sum_a, out_a)
    for c in range(chunks):
        cols = slice(c * width, (c + 1) * width)
        sums = jnp.dot(
            joined, ws_all[:, :, cols].reshape(-1, width), preferred_element_type=jnp.float32
        ) + jnp.dot(
            crossed, wc_all[:, :, cols].reshape(-1, width), preferred_element_type=jnp.float32
        )
        sum_v[:, cols] = sums.astype(jnp.bfloat16)
        deliver(1 + c, sum_v.at[:, cols], out_v.at[:, cols])

    @pl.when(w != h)
    def _():
        for away, here in last:
            away.wait()

    @pl.when(w == h)
    def _():
        for away, here in last:
            here.wait()

    for copy in list(a_copies.values()) + w_copies + f_copies + list(b_copies.values()):
        copy.wait_send()


def shards(*args):
    n = lax.axis_size("wide")
    count = lax.axis_size("heads")
    head_count = args[2].shape[1] // HDV
    if not (n == count == head_count and n % 2 == 0):
        return general_shards(*args)
    (video_hidden, audio_hidden, vq, vk, vv, aq, ak, av, cvq, cak, cav, caq, cvk, cvv,
     vso, vco, aso, aco, table) = args
    rows, few = vq.shape[0], aq.shape[0]
    blocks = jnp.arange(n, dtype=jnp.int32)
    offsets = blocks[None, :] - blocks[:, None] + REACH
    hits = offsets[:, :, None] == jnp.arange(table.shape[1], dtype=jnp.int32)
    allowed = jnp.any(hits & (table[:, None, :] > 0), axis=2)
    bias = jnp.where(allowed, 0.0, -1e30).astype(jnp.float32)
    bias_v = jnp.repeat(bias, few, axis=1)
    bias_a = jnp.repeat(bias.T, rows, axis=1)
    depth = rows + rows // 2 + 3 * few
    vmem = pl.BlockSpec(memory_space=pltpu.VMEM)
    anywhere = pl.BlockSpec(memory_space=pl.ANY)
    bf16 = jnp.bfloat16
    pack, wa = pl.pallas_call(
        functools.partial(pack_kernel, n),
        out_shape=(
            jax.ShapeDtypeStruct((n, depth, 2 * HDA), bf16),
            jax.ShapeDtypeStruct((2 * aso.shape[0], aso.shape[1]), bf16),
        ),
        in_specs=[vmem] * 11,
        out_specs=(vmem, vmem),
        name="pack",
    )(cvq, cvk, cvv, aq, ak, av, caq, cak, cav, aso, aco)
    chunks = max(1, vso.shape[1] // 256)
    rest = rows // 2 + few
    dma = pltpu.SemaphoreType.DMA
    video_sum, audio_sum = pl.pallas_call(
        functools.partial(fused_kernel, n, chunks),
        out_shape=(
            jax.ShapeDtypeStruct(video_hidden.shape, bf16),
            jax.ShapeDtypeStruct(audio_hidden.shape, bf16),
        ),
        in_specs=[anywhere] * 7 + [vmem] * 2,
        out_specs=(anywhere, anywhere),
        scratch_shapes=[
            pltpu.VMEM((n, rows, HDV), bf16),
            pltpu.VMEM((n, rows, HDV), bf16),
            pltpu.VMEM((n, rows, HDV), bf16),
            pltpu.VMEM((n, depth, 2 * HDA), bf16),
            pltpu.VMEM((n,) + vso.shape, bf16),
            pltpu.VMEM((n,) + vco.shape, bf16),
            pltpu.VMEM((n,) + wa.shape, bf16),
            pltpu.VMEM((n, rows, HDV), bf16),
            pltpu.VMEM((n, rest, 2 * HDA), bf16),
            pltpu.VMEM((n * n, rows, HDV), bf16),
            pltpu.VMEM((n * n, rest, 2 * HDA), bf16),
            pltpu.VMEM(video_hidden.shape, bf16),
            pltpu.VMEM(audio_hidden.shape, bf16),
            dma((4, n)), dma((4, n)),
            dma((3, n)), dma((3, n)),
            dma((3, n)), dma((3, n)),
            dma((2, n * n)), dma((2, n * n)),
            dma((1 + chunks,)), dma((1 + chunks,)),
            dma((8 + chunks,)),
        ],
        compiler_params=pltpu.CompilerParams(collective_id=0, has_side_effects=True),
        name="joint",
    )(vq, vk, vv, pack, vso, vco, wa, bias_v, bias_a)
    video_out = video_hidden.astype(jnp.float32) + video_sum.astype(jnp.float32)
    audio_out = audio_hidden.astype(jnp.float32) + audio_sum.astype(jnp.float32)
    return (video_out.astype(bf16), audio_out.astype(bf16))


def solution(mesh):
    placed = (
        P(("groups", "wide"), "heads"),
        P(("groups", "wide"), "heads"),
        P(("groups", "wide"), "heads"),
        P(("groups", "wide"), "heads"),
        P(("groups", "wide"), "heads"),
        P(("groups", "wide"), "heads"),
        P(("groups", "wide"), "heads"),
        P(("groups", "wide"), "heads"),
        P(("groups", "wide"), "heads"),
        P(("groups", "wide"), "heads"),
        P(("groups", "wide"), "heads"),
        P(("groups", "wide"), "heads"),
        P(("groups", "wide"), "heads"),
        P(("groups", "wide"), "heads"),
        P("heads", "wide"),
        P("heads", "wide"),
        P("heads", "wide"),
        P("heads", "wide"),
        P("groups", None),
    )
    return jax.shard_map(
        shards,
        mesh=mesh,
        in_specs=placed,
        out_specs=(P(("groups", "wide"), "heads"), P(("groups", "wide"), "heads")),
        check_vma=False,
    )
```

```python
import functools
import math

import jax
import jax.numpy as jnp
from jax import lax
from jax.experimental import pallas as pl
from jax.experimental.pallas import tpu as pltpu
from jax.sharding import PartitionSpec as P

HDV = 128
HDA = 64
REACH = 2


def passed_along(value, axis, by):
    length = lax.axis_size(axis)
    pairs = [(i, i + by) for i in range(length) if 0 <= i + by < length]
    return lax.ppermute(value, axis, pairs)


def empty_state(row_count, head_count, head_size):
    return (
        jnp.full((head_count, row_count), -1e30, jnp.float32),
        jnp.zeros((head_count, row_count), jnp.float32),
        jnp.zeros((head_count, row_count, head_size), jnp.float32),
    )


def absorb(state, queries, key_rows, value_rows, head_size, allowed):
    maxima, totals, running = state
    head_count = queries.shape[1] // head_size
    query_heads = queries.reshape(queries.shape[0], head_count, head_size)
    key_heads = key_rows.reshape(key_rows.shape[0], head_count, head_size)
    value_heads = value_rows.reshape(value_rows.shape[0], head_count, head_size)
    scores = jnp.einsum(
        "qhd,khd->hqk", query_heads, key_heads, preferred_element_type=jnp.float32
    ) * (1.0 / math.sqrt(head_size))
    if allowed is not None:
        scores = jnp.where(allowed[None, None, :], scores, -1e30)
    new_peak = jnp.maximum(maxima, jnp.max(scores, axis=2))
    weights = jnp.exp(scores - new_peak[:, :, None])
    if allowed is not None:
        weights = jnp.where(allowed[None, None, :], weights, 0.0)
    rescale = jnp.exp(maxima - new_peak)
    totals = totals * rescale + jnp.sum(weights, axis=2)
    running = running * rescale[:, :, None] + jnp.einsum(
        "hqk,khd->hqd",
        weights.astype(jnp.bfloat16),
        value_heads,
        preferred_element_type=jnp.float32,
    )
    return (new_peak, totals, running)


def finish(state, head_size):
    maxima, totals, running = state
    result = running / totals[:, :, None]
    return (
        result.transpose(1, 0, 2)
        .reshape(result.shape[1], result.shape[0] * head_size)
        .astype(jnp.bfloat16)
    )


def permitted(key_blocks, position, table_row, wide_count):
    offsets = key_blocks - position + REACH
    matches = (offsets[:, None] == jnp.arange(2 * REACH + 1, dtype=jnp.int32)[None, :]) & (
        table_row[None, :] > 0
    )
    inside = (key_blocks >= 0) & (key_blocks < wide_count)
    return jnp.any(matches, axis=1) & inside


def general_shards(
    video_hidden,
    audio_hidden,
    video_query,
    video_key,
    video_value,
    audio_query,
    audio_key,
    audio_value,
    cross_video_query,
    cross_audio_key,
    cross_audio_value,
    cross_audio_query,
    cross_video_key,
    cross_video_value,
    video_self_out,
    video_cross_out,
    audio_self_out,
    audio_cross_out,
    intersection,
):
    position = lax.axis_index("wide")
    wide_count = lax.axis_size("wide")
    video_count = video_query.shape[0]
    audio_count = audio_query.shape[0]
    head_count = video_query.shape[1] // HDV
    video_start = empty_state(video_count, head_count, HDV)
    audio_start = empty_state(audio_count, head_count, HDA)
    carried = (video_start, audio_start)
    portion = (
        lax.all_gather(video_key, "wide", axis=0, tiled=True),
        lax.all_gather(video_value, "wide", axis=0, tiled=True),
        lax.all_gather(audio_key, "wide", axis=0, tiled=True),
        lax.all_gather(audio_value, "wide", axis=0, tiled=True),
    )
    video_state = absorb(carried[0], video_query, portion[0], portion[1], HDV, None)
    audio_state = absorb(carried[1], audio_query, portion[2], portion[3], HDA, None)
    table_row = lax.dynamic_slice_in_dim(intersection, position, 1, 0)[0]
    padded_table = jnp.pad(intersection, ((REACH, REACH), (0, 0)))
    flag_row = jnp.diagonal(
        jnp.fliplr(lax.dynamic_slice_in_dim(padded_table, position, 2 * REACH + 1, 0))
    )
    stacked = jnp.concatenate(
        [cross_audio_key, cross_audio_value, cross_video_key, cross_video_value], 0
    )

    def take_cross(carried, portion, block):
        audio_keys = portion[:audio_count]
        audio_values = portion[audio_count : 2 * audio_count]
        video_keys = portion[2 * audio_count : 2 * audio_count + video_count]
        video_values = portion[2 * audio_count + video_count :]
        audio_blocks = jnp.full((audio_count,), block, jnp.int32)
        video_blocks = jnp.full((video_count,), block, jnp.int32)
        return (
            absorb(
                carried[0],
                cross_video_query,
                audio_keys,
                audio_values,
                HDA,
                permitted(audio_blocks, position, table_row, wide_count),
            ),
            absorb(
                carried[1],
                cross_audio_query,
                video_keys,
                video_values,
                HDA,
                permitted(video_blocks, position, flag_row, wide_count),
            ),
        )

    cross_start = (
        empty_state(video_count, head_count, HDA),
        empty_state(audio_count, head_count, HDA),
    )
    carried = take_cross(cross_start, stacked, position)
    for offset in range(-REACH, REACH + 1):
        if offset != 0:
            nearby = passed_along(stacked, "wide", -offset)
            carried = take_cross(carried, nearby, position + offset)
    to_video, to_audio = carried
    video_joined = jnp.concatenate([finish(video_state, HDV), finish(to_video, HDA)], 1)
    audio_joined = jnp.concatenate([finish(audio_state, HDA), finish(to_audio, HDA)], 1)
    video_weights = jnp.concatenate([video_self_out, video_cross_out], 0)
    audio_weights = jnp.concatenate([audio_self_out, audio_cross_out], 0)
    video_terms = jnp.dot(
        video_joined,
        lax.all_gather(video_weights, "wide", axis=1, tiled=True),
        preferred_element_type=jnp.float32,
    )
    audio_terms = jnp.dot(
        audio_joined,
        lax.all_gather(audio_weights, "wide", axis=1, tiled=True),
        preferred_element_type=jnp.float32,
    )
    video_sum, audio_sum = (
        lax.psum_scatter(
            video_terms.astype(jnp.bfloat16), "heads", scatter_dimension=1, tiled=True
        ).astype(jnp.float32),
        lax.psum_scatter(
            audio_terms.astype(jnp.bfloat16), "heads", scatter_dimension=1, tiled=True
        ).astype(jnp.float32),
    )
    video_out = (video_hidden.astype(jnp.float32) + video_sum).astype(jnp.bfloat16)
    audio_out = (audio_hidden.astype(jnp.float32) + audio_sum).astype(jnp.bfloat16)
    return (video_out, audio_out)


NT = (((1,), (1,)), ((), ()))
MESH = pl.DeviceIdType.MESH


def pack_kernel(
    n, cvq, cvk, cvv, aq, ak, av, caq, cak, cav, aso, aco, table, pack, wa, bias_v, bias_a
):
    rows = cvq.shape[0]
    half = rows // 2
    few = aq.shape[0]
    for i in range(n):
        for j in range(n):
            column = j - i + REACH
            drop = jnp.float32(-1e30)
            if 0 <= column < table.shape[1]:
                drop = jnp.where(table[i, column] > 0, jnp.float32(0.0), drop)
            bias_v[i : i + 1, j * few : (j + 1) * few] = jnp.full((1, few), drop)
            bias_a[j : j + 1, i * rows : (i + 1) * rows] = jnp.full((1, rows), drop)
    for j in range(n):
        cols = slice(j * HDA, (j + 1) * HDA)
        pack[j, :rows, :] = jnp.concatenate([cvq[:, cols], cvk[:, cols]], 1)
        pack[j, rows : rows + half, :] = jnp.concatenate([cvv[:half, cols], cvv[half:, cols]], 1)
        at = rows + half
        for left, right in ((aq, ak), (av, caq), (cak, cav)):
            pack[j, at : at + few, :] = jnp.concatenate([left[:, cols], right[:, cols]], 1)
            at += few
        wa[2 * j * HDA : (2 * j + 1) * HDA, :] = aso[cols, :]
        wa[(2 * j + 1) * HDA : (2 * j + 2) * HDA, :] = aco[cols, :]


def attend(queries, keys, values, head_size, bias):
    scores = lax.dot_general(queries, keys, NT, preferred_element_type=jnp.float32)
    scores = scores * (1.0 / math.sqrt(head_size))
    if bias is not None:
        scores = scores + bias
    weights = jnp.exp(scores - jnp.max(scores, axis=1, keepdims=True))
    totals = jnp.sum(weights, axis=1, keepdims=True)
    mixed = jnp.dot(weights.astype(jnp.bfloat16), values, preferred_element_type=jnp.float32)
    return (mixed / totals).astype(jnp.bfloat16)


def fused_kernel(
    n, chunks,
    vq, vk, vv, pack, ws, wc, wa, bias_v, bias_a,
    out_v, out_a,
    q_all, k_all, v_all, p_all, ws_all, wc_all, wa_all,
    o_self, o_rest, r_self, r_rest, sum_v, sum_a, mid_v, mid_a,
    a_send, a_recv, w_send, w_recv, f_send, f_recv, x_send, x_recv, z_send, z_recv,
    d_send, d_recv, e_send, e_recv, local,
):
    w = lax.axis_index("wide")
    h = lax.axis_index("heads")
    rows = vq.shape[0]
    half = rows // 2
    few = out_a.shape[0]
    part_rows, part_few = rows // n, few // n

    def place(dw, dh):
        return {"wide": lax.rem(w + dw, n), "heads": lax.rem(h + dh, n)}

    def remote(source, target, send, recv, device):
        return pltpu.make_async_remote_copy(
            src_ref=source, dst_ref=target, send_sem=send, recv_sem=recv,
            device_id=device, device_id_type=MESH,
        )

    others = [(d, 0) for d in range(1, n)] + [(0, d) for d in range(1, n)]
    barrier = pltpu.get_barrier_semaphore()
    for dw, dh in others:
        pl.semaphore_signal(barrier, inc=1, device_id=place(dw, dh), device_id_type=MESH)

    def head_cols(ref, who):
        return ref.at[:, pl.ds(pl.multiple_of(who * HDV, HDV), HDV)]

    own = [pltpu.make_async_copy(pack.at[w], p_all.at[w], local.at[0])]
    for i, (source, target) in enumerate(((vk, k_all), (vv, v_all), (vq, q_all))):
        own.append(pltpu.make_async_copy(head_cols(source, w), target.at[w], local.at[1 + i]))
    for i, (source, target) in enumerate(((ws, ws_all), (wc, wc_all), (wa, wa_all))):
        own.append(pltpu.make_async_copy(source, target.at[h], local.at[4 + i]))
    for copy in own:
        copy.start()
    pl.semaphore_wait(barrier, len(others))

    a_copies = {}
    for i, (source, target) in enumerate(((pack, p_all), (vk, k_all), (vv, v_all), (vq, q_all))):
        for d in range(1, n):
            who = lax.rem(w + d, n)
            piece = source.at[who] if i == 0 else head_cols(source, who)
            copy = remote(piece, target.at[w], a_send.at[i, d], a_recv.at[i, d], place(d, 0))
            copy.start()
            a_copies[i, d] = copy

    pairs = ((ws, ws_all), (wc, wc_all), (wa, wa_all))
    partner = {"wide": w, "heads": h + 1 - 2 * lax.rem(h, 2)}
    w_copies, f_copies = [], []
    for i, (source, target) in enumerate(pairs):
        for k in range(1, n // 2):
            copy = remote(source, target.at[h], w_send.at[i, k], w_recv.at[i, k], place(0, 2 * k))
            copy.start()
            w_copies.append(copy)
        copy = remote(source, target.at[h], f_send.at[i, 0], f_recv.at[i, 0], partner)
        copy.start()
        f_copies.append(copy)

    own[0].wait()
    for d in range(1, n):
        a_copies[0, d].wait_recv()
    at = rows + half

    def part(j, start, right):
        return p_all[j, start : start + few, HDA:] if right else p_all[j, start : start + few, :HDA]

    def whole(start, right):
        return jnp.concatenate([part(j, start, right) for j in range(n)], 0)

    aq, ak = whole(at, False), whole(at, True)
    av, caq = whole(at + few, False), whole(at + few, True)
    cak, cav = whole(at + 2 * few, False), whole(at + 2 * few, True)
    cvk = jnp.concatenate([p_all[j, :rows, HDA:] for j in range(n)], 0)
    cvv = jnp.concatenate(
        [p_all[j, rows:at, cols] for j in range(n) for cols in (slice(0, HDA), slice(HDA, 2 * HDA))], 0
    )
    wide_bias = jnp.concatenate(
        [jnp.broadcast_to(bias_a[j : j + 1, :], (few, bias_a.shape[1])) for j in range(n)], 0
    )
    audio = jnp.concatenate(
        [attend(aq, ak, av, HDA, None), attend(caq, cvk, cvv, HDA, wide_bias)], 1
    )
    tall_bias = jnp.concatenate(
        [jnp.broadcast_to(bias_v[j : j + 1, :], (part_rows, bias_v.shape[1])) for j in range(n)], 0
    )
    for t in range(n):
        queries = jnp.concatenate(
            [p_all[j, t * part_rows : (t + 1) * part_rows, :HDA] for j in range(n)], 0
        )
        o_rest[t, half:, :] = jnp.concatenate(
            [audio[j * few + t * part_few : j * few + (t + 1) * part_few, :] for j in range(n)], 0
        )
        mixed = attend(queries, cak, cav, HDA, tall_bias)
        o_rest[t, :half, :] = jnp.concatenate([mixed[:half], mixed[half:]], 1)

    mine = h * n + w
    buffers = ((o_rest, r_rest), (o_self, r_self))
    x_copies = {}
    steps = n - 1

    def across(kind, d):
        source, landing = buffers[kind]
        copy = remote(
            source.at[lax.rem(h + d, n)], landing.at[mine],
            x_send.at[kind, d], x_recv.at[kind, d], place(0, d),
        )
        copy.start()
        x_copies[kind, d] = copy

    def along(kind, d, step, way):
        source, landing = buffers[kind]
        slot = lax.rem(h + n - d, n) * n + w - way * step
        piece = source.at[h] if d == 0 and step == 0 else landing.at[slot]
        at = (((way + 1) // 2 * steps + step) * 2 + kind) * n + d
        return remote(
            piece, landing.at[slot], z_send.at[at], z_recv.at[at],
            {"wide": w + way, "heads": h},
        )

    def sends(step, way):
        if way > 0:
            return (w >= step) & (w < n - 1)
        return (w + step < n) & (w > 0)

    def forward(kind, d, step):
        for way in (1, -1):
            if step:
                gather(kind, d, step - 1, way)

            @pl.when(sends(step, way))
            def _():
                along(kind, d, step, way).start()

    def gather(kind, d, step, way):
        arrives = (w >= step + 1) if way > 0 else (w + step + 1 < n)

        @pl.when(arrives)
        def _():
            landing = buffers[kind][1]
            at = (((way + 1) // 2 * steps + step) * 2 + kind) * n + d
            slot = lax.rem(h + n - d, n) * n + w - way * (step + 1)
            remote(
                landing.at[slot], landing.at[slot], z_send.at[at], z_recv.at[at],
                {"wide": w - way, "heads": h},
            ).wait_recv()

    for d in range(1, n):
        across(0, d)
    forward(0, 0, 0)
    r_rest[pl.ds(mine, 1)] = o_rest[pl.ds(h, 1)]
    for d in range(1, n):
        x_copies[0, d].wait_recv()
        forward(0, d, 0)

    for i in range(1, 4):
        own[i].wait()
        for d in range(1, n):
            a_copies[i, d].wait_recv()
    keys = k_all[...].reshape(n * rows, HDV)
    values = v_all[...].reshape(n * rows, HDV)
    for d in range(n):
        block = lax.rem(h + d, n)
        start = pl.multiple_of(block * part_rows, part_rows)
        queries = q_all[:, pl.ds(start, part_rows), :].reshape(rows, HDV)
        o_self[pl.ds(block, 1)] = attend(queries, keys, values, HDV, None)[None]
        if d:
            across(1, d)
        else:
            forward(1, 0, 0)
            r_self[pl.ds(mine, 1)] = o_self[pl.ds(h, 1)]
        if d > 1:
            x_copies[1, d - 1].wait_recv()
            forward(1, d - 1, 0)
        if steps > 1:
            forward(0, d, 1)
    x_copies[1, n - 1].wait_recv()
    forward(1, n - 1, 0)

    for copy in w_copies:
        copy.wait_recv()
    for i, (source, target) in enumerate(pairs):
        for k in range(1, n // 2):
            slot = lax.rem(h + n - 2 * k, n)
            copy = remote(target.at[slot], target.at[slot], f_send.at[i, k], f_recv.at[i, k], partner)
            copy.start()
            f_copies.append(copy)

    for kind in range(2):
        for step in range(2 - kind, steps):
            for d in range(n):
                forward(kind, d, step)
    for kind in range(2):
        for d in range(n):
            for way in (1, -1):
                gather(kind, d, steps - 1, way)

    for copy in own[4:]:
        copy.wait()
    for copy in f_copies:
        copy.wait_recv()

    heads = n * n
    joined = jnp.concatenate([r_self[s] for s in range(heads)], 1)
    crossed = jnp.concatenate(
        [
            jnp.concatenate([r_rest[s, :half, :HDA] for s in range(heads)], 1),
            jnp.concatenate([r_rest[s, :half, HDA:] for s in range(heads)], 1),
        ],
        0,
    )
    audio_joined = jnp.concatenate([r_rest[s, half:, :] for s in range(heads)], 1)
    width = ws.shape[1] // chunks
    audio_width = wa.shape[1]

    def piece(ref, c):
        return ref if c == 0 else ref.at[:, (c - 1) * width : c * width]

    def rows_of(ref, c, block):
        size = part_few if c == 0 else part_rows
        return piece(ref.at[pl.ds(pl.multiple_of(block * size, size), size)], c)

    def first_hop(c):
        source, middle = (sum_a, mid_a) if c == 0 else (sum_v, mid_v)
        for d in range(1, n):
            copy = remote(
                rows_of(source, c, lax.rem(w + d, n)), piece(middle.at[w], c),
                d_send.at[c, d], d_recv.at[c, d], place(d, 0),
            )
            copy.start()
            d_copies[c, d] = copy

    def second_hop(c, d):
        source, middle, out = (sum_a, mid_a, out_a) if c == 0 else (sum_v, mid_v, out_v)
        origin = lax.rem(w + n - d, n)
        ready = piece(middle.at[origin], c) if d else rows_of(source, c, w)
        target = rows_of(out, c, h)
        away = remote(
            ready, target, e_send.at[c, d], e_recv.at[c, lax.rem(origin + n - h, n)],
            {"wide": w, "heads": origin},
        )
        here = pltpu.make_async_copy(ready, target, local.at[7 + c])

        @pl.when(origin != h)
        def _():
            away.start()

        @pl.when(origin == h)
        def _():
            here.start()

        last.append((origin, away, here))

    d_copies, last = {}, []
    order = list(range(1, chunks + 1)) + [0]
    for c in order:
        if c:
            cols = slice((c - 1) * width, c * width)
            sums = jnp.dot(
                joined, ws_all[:, :, cols].reshape(-1, width), preferred_element_type=jnp.float32
            ) + jnp.dot(
                crossed, wc_all[:, :, cols].reshape(-1, width), preferred_element_type=jnp.float32
            )
            sum_v[:, cols] = sums.astype(jnp.bfloat16)
        else:
            sums = jnp.dot(
                audio_joined, wa_all[...].reshape(-1, audio_width),
                preferred_element_type=jnp.float32,
            )
            sum_a[...] = sums.astype(jnp.bfloat16)
        first_hop(c)
        second_hop(c, 0)
    for c in order:
        for d in range(1, n):
            d_copies[c, d].wait_recv()
            second_hop(c, d)

    for origin, away, here in last:
        @pl.when(origin != h)
        def _():
            away.wait_send()

        @pl.when(origin == h)
        def _():
            here.wait()

    for c in order:
        out = out_a if c == 0 else out_v
        for d in range(1, n):
            who = lax.rem(h + d, n)
            target = rows_of(out, c, who)
            remote(
                target, target, e_send.at[c, 0], e_recv.at[c, n - d],
                {"wide": w, "heads": who},
            ).wait_recv()

    for copy in (
        list(a_copies.values()) + w_copies + f_copies
        + list(x_copies.values()) + list(d_copies.values())
    ):
        copy.wait_send()
    for step in range(steps):
        for way in (1, -1):
            @pl.when(sends(step, way))
            def _():
                for kind in range(2):
                    for d in range(n):
                        along(kind, d, step, way).wait_send()


def shards(*args):
    n = lax.axis_size("wide")
    count = lax.axis_size("heads")
    head_count = args[2].shape[1] // HDV
    if not (n == count == head_count and n % 2 == 0 and args[5].shape[0] % (16 * n) == 0):
        return general_shards(*args)
    (video_hidden, audio_hidden, vq, vk, vv, aq, ak, av, cvq, cak, cav, caq, cvk, cvv,
     vso, vco, aso, aco, table) = args
    rows, few = vq.shape[0], aq.shape[0]
    depth = rows + rows // 2 + 3 * few
    vmem = pl.BlockSpec(memory_space=pltpu.VMEM)
    anywhere = pl.BlockSpec(memory_space=pl.ANY)
    bf16 = jnp.bfloat16
    pack, wa, bias_v, bias_a = pl.pallas_call(
        functools.partial(pack_kernel, n),
        out_shape=(
            jax.ShapeDtypeStruct((n, depth, 2 * HDA), bf16),
            jax.ShapeDtypeStruct((2 * aso.shape[0], aso.shape[1]), bf16),
            jax.ShapeDtypeStruct((n, n * few), jnp.float32),
            jax.ShapeDtypeStruct((n, n * rows), jnp.float32),
        ),
        in_specs=[vmem] * 11 + [pl.BlockSpec(memory_space=pltpu.SMEM)],
        out_specs=(vmem, vmem, vmem, vmem),
        name="pack",
    )(cvq, cvk, cvv, aq, ak, av, caq, cak, cav, aso, aco, table)
    chunks = max(1, vso.shape[1] // 512)
    rest = rows // 2 + few
    dma = pltpu.SemaphoreType.DMA
    video_sum, audio_sum = pl.pallas_call(
        functools.partial(fused_kernel, n, chunks),
        out_shape=(
            jax.ShapeDtypeStruct(video_hidden.shape, bf16),
            jax.ShapeDtypeStruct(audio_hidden.shape, bf16),
        ),
        in_specs=[anywhere] * 7 + [vmem] * 2,
        out_specs=(anywhere, anywhere),
        scratch_shapes=[
            pltpu.VMEM((n, rows, HDV), bf16),
            pltpu.VMEM((n, rows, HDV), bf16),
            pltpu.VMEM((n, rows, HDV), bf16),
            pltpu.VMEM((n, depth, 2 * HDA), bf16),
            pltpu.VMEM((n,) + vso.shape, bf16),
            pltpu.VMEM((n,) + vco.shape, bf16),
            pltpu.VMEM((n,) + wa.shape, bf16),
            pltpu.VMEM((n, rows, HDV), bf16),
            pltpu.VMEM((n, rest, 2 * HDA), bf16),
            pltpu.VMEM((n * n, rows, HDV), bf16),
            pltpu.VMEM((n * n, rest, 2 * HDA), bf16),
            pltpu.VMEM(video_hidden.shape, bf16),
            pltpu.VMEM(audio_hidden.shape, bf16),
            pltpu.VMEM((n, rows // n, video_hidden.shape[1]), bf16),
            pltpu.VMEM((n, few // n, audio_hidden.shape[1]), bf16),
            dma((4, n)), dma((4, n)),
            dma((3, n)), dma((3, n)),
            dma((3, n)), dma((3, n)),
            dma((2, n)), dma((2, n)),
            dma((4 * n * (n - 1),)), dma((4 * n * (n - 1),)),
            dma((1 + chunks, n)), dma((1 + chunks, n)),
            dma((1 + chunks, n)), dma((1 + chunks, n)),
            dma((8 + chunks,)),
        ],
        compiler_params=pltpu.CompilerParams(collective_id=0, has_side_effects=True),
        name="joint",
    )(vq, vk, vv, pack, vso, vco, wa, bias_v, bias_a)
    video_out = video_hidden.astype(jnp.float32) + video_sum.astype(jnp.float32)
    audio_out = audio_hidden.astype(jnp.float32) + audio_sum.astype(jnp.float32)
    return (video_out.astype(bf16), audio_out.astype(bf16))


def solution(mesh):
    placed = (
        P(("groups", "wide"), "heads"),
        P(("groups", "wide"), "heads"),
        P(("groups", "wide"), "heads"),
        P(("groups", "wide"), "heads"),
        P(("groups", "wide"), "heads"),
        P(("groups", "wide"), "heads"),
        P(("groups", "wide"), "heads"),
        P(("groups", "wide"), "heads"),
        P(("groups", "wide"), "heads"),
        P(("groups", "wide"), "heads"),
        P(("groups", "wide"), "heads"),
        P(("groups", "wide"), "heads"),
        P(("groups", "wide"), "heads"),
        P(("groups", "wide"), "heads"),
        P("heads", "wide"),
        P("heads", "wide"),
        P("heads", "wide"),
        P("heads", "wide"),
        P("groups", None),
    )
    return jax.shard_map(
        shards,
        mesh=mesh,
        in_specs=placed,
        out_specs=(P(("groups", "wide"), "heads"), P(("groups", "wide"), "heads")),
        check_vma=False,
    )
```

```python
import functools
import math

import jax
import jax.numpy as jnp
from jax import lax
from jax.experimental import pallas as pl
from jax.experimental.pallas import tpu as pltpu
from jax.sharding import PartitionSpec as P

HDV = 128
HDA = 64
REACH = 2


def passed_along(value, axis, by):
    length = lax.axis_size(axis)
    pairs = [(i, i + by) for i in range(length) if 0 <= i + by < length]
    return lax.ppermute(value, axis, pairs)


def empty_state(row_count, head_count, head_size):
    return (
        jnp.full((head_count, row_count), -1e30, jnp.float32),
        jnp.zeros((head_count, row_count), jnp.float32),
        jnp.zeros((head_count, row_count, head_size), jnp.float32),
    )


def absorb(state, queries, key_rows, value_rows, head_size, allowed):
    maxima, totals, running = state
    head_count = queries.shape[1] // head_size
    query_heads = queries.reshape(queries.shape[0], head_count, head_size)
    key_heads = key_rows.reshape(key_rows.shape[0], head_count, head_size)
    value_heads = value_rows.reshape(value_rows.shape[0], head_count, head_size)
    scores = jnp.einsum(
        "qhd,khd->hqk", query_heads, key_heads, preferred_element_type=jnp.float32
    ) * (1.0 / math.sqrt(head_size))
    if allowed is not None:
        scores = jnp.where(allowed[None, None, :], scores, -1e30)
    new_peak = jnp.maximum(maxima, jnp.max(scores, axis=2))
    weights = jnp.exp(scores - new_peak[:, :, None])
    if allowed is not None:
        weights = jnp.where(allowed[None, None, :], weights, 0.0)
    rescale = jnp.exp(maxima - new_peak)
    totals = totals * rescale + jnp.sum(weights, axis=2)
    running = running * rescale[:, :, None] + jnp.einsum(
        "hqk,khd->hqd",
        weights.astype(jnp.bfloat16),
        value_heads,
        preferred_element_type=jnp.float32,
    )
    return (new_peak, totals, running)


def finish(state, head_size):
    maxima, totals, running = state
    result = running / totals[:, :, None]
    return (
        result.transpose(1, 0, 2)
        .reshape(result.shape[1], result.shape[0] * head_size)
        .astype(jnp.bfloat16)
    )


def permitted(key_blocks, position, table_row, wide_count):
    offsets = key_blocks - position + REACH
    matches = (offsets[:, None] == jnp.arange(2 * REACH + 1, dtype=jnp.int32)[None, :]) & (
        table_row[None, :] > 0
    )
    inside = (key_blocks >= 0) & (key_blocks < wide_count)
    return jnp.any(matches, axis=1) & inside


def general_shards(
    video_hidden,
    audio_hidden,
    video_query,
    video_key,
    video_value,
    audio_query,
    audio_key,
    audio_value,
    cross_video_query,
    cross_audio_key,
    cross_audio_value,
    cross_audio_query,
    cross_video_key,
    cross_video_value,
    video_self_out,
    video_cross_out,
    audio_self_out,
    audio_cross_out,
    intersection,
):
    position = lax.axis_index("wide")
    wide_count = lax.axis_size("wide")
    video_count = video_query.shape[0]
    audio_count = audio_query.shape[0]
    head_count = video_query.shape[1] // HDV
    video_start = empty_state(video_count, head_count, HDV)
    audio_start = empty_state(audio_count, head_count, HDA)
    carried = (video_start, audio_start)
    portion = (
        lax.all_gather(video_key, "wide", axis=0, tiled=True),
        lax.all_gather(video_value, "wide", axis=0, tiled=True),
        lax.all_gather(audio_key, "wide", axis=0, tiled=True),
        lax.all_gather(audio_value, "wide", axis=0, tiled=True),
    )
    video_state = absorb(carried[0], video_query, portion[0], portion[1], HDV, None)
    audio_state = absorb(carried[1], audio_query, portion[2], portion[3], HDA, None)
    table_row = lax.dynamic_slice_in_dim(intersection, position, 1, 0)[0]
    padded_table = jnp.pad(intersection, ((REACH, REACH), (0, 0)))
    flag_row = jnp.diagonal(
        jnp.fliplr(lax.dynamic_slice_in_dim(padded_table, position, 2 * REACH + 1, 0))
    )
    stacked = jnp.concatenate(
        [cross_audio_key, cross_audio_value, cross_video_key, cross_video_value], 0
    )

    def take_cross(carried, portion, block):
        audio_keys = portion[:audio_count]
        audio_values = portion[audio_count : 2 * audio_count]
        video_keys = portion[2 * audio_count : 2 * audio_count + video_count]
        video_values = portion[2 * audio_count + video_count :]
        audio_blocks = jnp.full((audio_count,), block, jnp.int32)
        video_blocks = jnp.full((video_count,), block, jnp.int32)
        return (
            absorb(
                carried[0],
                cross_video_query,
                audio_keys,
                audio_values,
                HDA,
                permitted(audio_blocks, position, table_row, wide_count),
            ),
            absorb(
                carried[1],
                cross_audio_query,
                video_keys,
                video_values,
                HDA,
                permitted(video_blocks, position, flag_row, wide_count),
            ),
        )

    cross_start = (
        empty_state(video_count, head_count, HDA),
        empty_state(audio_count, head_count, HDA),
    )
    carried = take_cross(cross_start, stacked, position)
    for offset in range(-REACH, REACH + 1):
        if offset != 0:
            nearby = passed_along(stacked, "wide", -offset)
            carried = take_cross(carried, nearby, position + offset)
    to_video, to_audio = carried
    video_joined = jnp.concatenate([finish(video_state, HDV), finish(to_video, HDA)], 1)
    audio_joined = jnp.concatenate([finish(audio_state, HDA), finish(to_audio, HDA)], 1)
    video_weights = jnp.concatenate([video_self_out, video_cross_out], 0)
    audio_weights = jnp.concatenate([audio_self_out, audio_cross_out], 0)
    video_terms = jnp.dot(
        video_joined,
        lax.all_gather(video_weights, "wide", axis=1, tiled=True),
        preferred_element_type=jnp.float32,
    )
    audio_terms = jnp.dot(
        audio_joined,
        lax.all_gather(audio_weights, "wide", axis=1, tiled=True),
        preferred_element_type=jnp.float32,
    )
    video_sum, audio_sum = (
        lax.psum_scatter(
            video_terms.astype(jnp.bfloat16), "heads", scatter_dimension=1, tiled=True
        ).astype(jnp.float32),
        lax.psum_scatter(
            audio_terms.astype(jnp.bfloat16), "heads", scatter_dimension=1, tiled=True
        ).astype(jnp.float32),
    )
    video_out = (video_hidden.astype(jnp.float32) + video_sum).astype(jnp.bfloat16)
    audio_out = (audio_hidden.astype(jnp.float32) + audio_sum).astype(jnp.bfloat16)
    return (video_out, audio_out)


NT = (((1,), (1,)), ((), ()))
MESH = pl.DeviceIdType.MESH


def pack_kernel(
    n, cvq, cvk, cvv, aq, ak, av, caq, cak, cav, aso, aco, table, pack, wa, bias_v, bias_a
):
    rows = cvq.shape[0]
    half = rows // 2
    few = aq.shape[0]
    for i in range(n):
        for j in range(n):
            column = j - i + REACH
            drop = jnp.float32(-1e30)
            if 0 <= column < table.shape[1]:
                drop = jnp.where(table[i, column] > 0, jnp.float32(0.0), drop)
            bias_v[i : i + 1, j * few : (j + 1) * few] = jnp.full((1, few), drop)
            bias_a[j : j + 1, i * rows : (i + 1) * rows] = jnp.full((1, rows), drop)
    for j in range(n):
        cols = slice(j * HDA, (j + 1) * HDA)
        pack[j, :rows, :] = jnp.concatenate([cvq[:, cols], cvk[:, cols]], 1)
        pack[j, rows : rows + half, :] = jnp.concatenate([cvv[:half, cols], cvv[half:, cols]], 1)
        at = rows + half
        for left, right in ((aq, ak), (av, caq), (cak, cav)):
            pack[j, at : at + few, :] = jnp.concatenate([left[:, cols], right[:, cols]], 1)
            at += few
        wa[2 * j * HDA : (2 * j + 1) * HDA, :] = aso[cols, :]
        wa[(2 * j + 1) * HDA : (2 * j + 2) * HDA, :] = aco[cols, :]


def attend(queries, keys, values, head_size, bias):
    scores = lax.dot_general(queries, keys, NT, preferred_element_type=jnp.float32)
    scores = scores * (1.0 / math.sqrt(head_size))
    if bias is not None:
        scores = scores + bias
    weights = jnp.exp(scores - jnp.max(scores, axis=1, keepdims=True))
    totals = jnp.sum(weights, axis=1, keepdims=True)
    mixed = jnp.dot(weights.astype(jnp.bfloat16), values, preferred_element_type=jnp.float32)
    return (mixed / totals).astype(jnp.bfloat16)


def fused_kernel(
    n, chunks,
    vq, vk, vv, pack, ws, wc, wa, bias_v, bias_a,
    out_v, out_a,
    q_all, k_all, v_all, p_all, ws_all, wc_all, wa_all,
    o_self, o_rest, r_self, r_rest, sum_v, sum_a, mid_v, mid_a,
    a_send, a_recv, w_send, w_recv, f_send, f_recv, x_send, x_recv, z_send, z_recv,
    d_send, d_recv, e_send, e_recv, local,
):
    w = lax.axis_index("wide")
    h = lax.axis_index("heads")
    rows = vq.shape[0]
    half = rows // 2
    few = out_a.shape[0]
    part_rows, part_few = rows // n, few // n

    def place(dw, dh):
        return {"wide": lax.rem(w + dw, n), "heads": lax.rem(h + dh, n)}

    def remote(source, target, send, recv, device):
        return pltpu.make_async_remote_copy(
            src_ref=source, dst_ref=target, send_sem=send, recv_sem=recv,
            device_id=device, device_id_type=MESH,
        )

    others = [(d, 0) for d in range(1, n)] + [(0, d) for d in range(1, n)]
    barrier = pltpu.get_barrier_semaphore()
    for dw, dh in others:
        pl.semaphore_signal(barrier, inc=1, device_id=place(dw, dh), device_id_type=MESH)

    def head_cols(ref, who):
        return ref.at[:, pl.ds(pl.multiple_of(who * HDV, HDV), HDV)]

    own = [pltpu.make_async_copy(pack.at[w], p_all.at[w], local.at[0])]
    for i, (source, target) in enumerate(((vk, k_all), (vv, v_all), (vq, q_all))):
        own.append(pltpu.make_async_copy(head_cols(source, w), target.at[w], local.at[1 + i]))
    for i, (source, target) in enumerate(((ws, ws_all), (wc, wc_all), (wa, wa_all))):
        own.append(pltpu.make_async_copy(source, target.at[h], local.at[4 + i]))
    for copy in own:
        copy.start()
    pl.semaphore_wait(barrier, len(others))

    a_copies = {}
    for i, (source, target) in enumerate(((pack, p_all), (vk, k_all), (vv, v_all), (vq, q_all))):
        for d in range(1, n):
            who = lax.rem(w + d, n)
            piece = source.at[who] if i == 0 else head_cols(source, who)
            copy = remote(piece, target.at[w], a_send.at[i, d], a_recv.at[i, d], place(d, 0))
            copy.start()
            a_copies[i, d] = copy

    pairs = ((ws, ws_all), (wc, wc_all), (wa, wa_all))
    partner = {"wide": w, "heads": h + 1 - 2 * lax.rem(h, 2)}
    w_copies, f_copies = [[], [], []], [[], [], []]

    def send_weights(i):
        source, target = pairs[i]
        for k in range(1, n // 2):
            copy = remote(source, target.at[h], w_send.at[i, k], w_recv.at[i, k], place(0, 2 * k))
            copy.start()
            w_copies[i].append(copy)

    def pass_weights(i):
        target = pairs[i][1]
        for k in range(1, n // 2):
            w_copies[i][k - 1].wait_recv()
            slot = lax.rem(h + n - 2 * k, n)
            copy = remote(target.at[slot], target.at[slot], f_send.at[i, k], f_recv.at[i, k], partner)
            copy.start()
            f_copies[i].append(copy)

    def settle_weights(i):
        own[4 + i].wait()
        for copy in f_copies[i]:
            copy.wait_recv()

    send_weights(0)
    for i, (source, target) in enumerate(pairs):
        copy = remote(source, target.at[h], f_send.at[i, 0], f_recv.at[i, 0], partner)
        copy.start()
        f_copies[i].append(copy)

    own[0].wait()
    for d in range(1, n):
        a_copies[0, d].wait_recv()
    at = rows + half

    def part(j, start, right):
        return p_all[j, start : start + few, HDA:] if right else p_all[j, start : start + few, :HDA]

    def whole(start, right):
        return jnp.concatenate([part(j, start, right) for j in range(n)], 0)

    aq, ak = whole(at, False), whole(at, True)
    av, caq = whole(at + few, False), whole(at + few, True)
    cak, cav = whole(at + 2 * few, False), whole(at + 2 * few, True)
    cvk = jnp.concatenate([p_all[j, :rows, HDA:] for j in range(n)], 0)
    cvv = jnp.concatenate(
        [p_all[j, rows:at, cols] for j in range(n) for cols in (slice(0, HDA), slice(HDA, 2 * HDA))], 0
    )
    wide_bias = jnp.concatenate(
        [jnp.broadcast_to(bias_a[j : j + 1, :], (few, bias_a.shape[1])) for j in range(n)], 0
    )
    audio = jnp.concatenate(
        [attend(aq, ak, av, HDA, None), attend(caq, cvk, cvv, HDA, wide_bias)], 1
    )
    tall_bias = jnp.concatenate(
        [jnp.broadcast_to(bias_v[j : j + 1, :], (part_rows, bias_v.shape[1])) for j in range(n)], 0
    )
    for t in range(n):
        queries = jnp.concatenate(
            [p_all[j, t * part_rows : (t + 1) * part_rows, :HDA] for j in range(n)], 0
        )
        o_rest[t, half:, :] = jnp.concatenate(
            [audio[j * few + t * part_few : j * few + (t + 1) * part_few, :] for j in range(n)], 0
        )
        mixed = attend(queries, cak, cav, HDA, tall_bias)
        o_rest[t, :half, :] = jnp.concatenate([mixed[:half], mixed[half:]], 1)

    mine = h * n + w
    buffers = ((o_rest, r_rest), (o_self, r_self))
    x_copies = {}
    steps = n - 1

    def across(kind, d):
        source, landing = buffers[kind]
        copy = remote(
            source.at[lax.rem(h + d, n)], landing.at[mine],
            x_send.at[kind, d], x_recv.at[kind, d], place(0, d),
        )
        copy.start()
        x_copies[kind, d] = copy

    def along(kind, d, step, way):
        source, landing = buffers[kind]
        slot = lax.rem(h + n - d, n) * n + w - way * step
        piece = source.at[h] if d == 0 and step == 0 else landing.at[slot]
        at = (((way + 1) // 2 * steps + step) * 2 + kind) * n + d
        return remote(
            piece, landing.at[slot], z_send.at[at], z_recv.at[at],
            {"wide": w + way, "heads": h},
        )

    def sends(step, way):
        if way > 0:
            return (w >= step) & (w < n - 1)
        return (w + step < n) & (w > 0)

    def forward(kind, d, step):
        for way in (1, -1):
            if step:
                gather(kind, d, step - 1, way)

            @pl.when(sends(step, way))
            def _():
                along(kind, d, step, way).start()

    def gather(kind, d, step, way):
        arrives = (w >= step + 1) if way > 0 else (w + step + 1 < n)

        @pl.when(arrives)
        def _():
            landing = buffers[kind][1]
            at = (((way + 1) // 2 * steps + step) * 2 + kind) * n + d
            slot = lax.rem(h + n - d, n) * n + w - way * (step + 1)
            remote(
                landing.at[slot], landing.at[slot], z_send.at[at], z_recv.at[at],
                {"wide": w - way, "heads": h},
            ).wait_recv()

    for d in range(1, n):
        across(0, d)
    send_weights(1)
    forward(0, 0, 0)
    r_rest[pl.ds(mine, 1)] = o_rest[pl.ds(h, 1)]
    for d in range(1, n):
        x_copies[0, d].wait_recv()
        forward(0, d, 0)

    for i in range(1, 4):
        own[i].wait()
        for d in range(1, n):
            a_copies[i, d].wait_recv()
    keys = k_all[...].reshape(n * rows, HDV)
    values = v_all[...].reshape(n * rows, HDV)
    for d in range(n):
        block = lax.rem(h + d, n)
        start = pl.multiple_of(block * part_rows, part_rows)
        queries = q_all[:, pl.ds(start, part_rows), :].reshape(rows, HDV)
        o_self[pl.ds(block, 1)] = attend(queries, keys, values, HDV, None)[None]
        if d:
            across(1, d)
        else:
            forward(1, 0, 0)
            r_self[pl.ds(mine, 1)] = o_self[pl.ds(h, 1)]
        if d > 1:
            x_copies[1, d - 1].wait_recv()
            forward(1, d - 1, 0)
        if steps > 1:
            forward(0, d, 1)
    x_copies[1, n - 1].wait_recv()
    forward(1, n - 1, 0)

    send_weights(2)
    pass_weights(0)
    pass_weights(1)

    for kind in range(2):
        for step in range(2 - kind, steps):
            for d in range(n):
                forward(kind, d, step)
    for kind in range(2):
        for d in range(n):
            for way in (1, -1):
                gather(kind, d, steps - 1, way)

    pass_weights(2)
    settle_weights(0)
    settle_weights(1)

    heads = n * n
    joined = jnp.concatenate([r_self[s] for s in range(heads)], 1)
    crossed = jnp.concatenate(
        [
            jnp.concatenate([r_rest[s, :half, :HDA] for s in range(heads)], 1),
            jnp.concatenate([r_rest[s, :half, HDA:] for s in range(heads)], 1),
        ],
        0,
    )
    audio_joined = jnp.concatenate([r_rest[s, half:, :] for s in range(heads)], 1)
    width = ws.shape[1] // chunks
    audio_width = wa.shape[1]

    def piece(ref, c):
        return ref if c == 0 else ref.at[:, (c - 1) * width : c * width]

    def rows_of(ref, c, block):
        size = part_few if c == 0 else part_rows
        return piece(ref.at[pl.ds(pl.multiple_of(block * size, size), size)], c)

    def first_hop(c):
        source, middle = (sum_a, mid_a) if c == 0 else (sum_v, mid_v)
        for d in range(1, n):
            copy = remote(
                rows_of(source, c, lax.rem(w + d, n)), piece(middle.at[w], c),
                d_send.at[c, d], d_recv.at[c, d], place(d, 0),
            )
            copy.start()
            d_copies[c, d] = copy

    def second_hop(c, d):
        source, middle, out = (sum_a, mid_a, out_a) if c == 0 else (sum_v, mid_v, out_v)
        origin = lax.rem(w + n - d, n)
        ready = piece(middle.at[origin], c) if d else rows_of(source, c, w)
        target = rows_of(out, c, h)
        away = remote(
            ready, target, e_send.at[c, d], e_recv.at[c, lax.rem(origin + n - h, n)],
            {"wide": w, "heads": origin},
        )
        here = pltpu.make_async_copy(ready, target, local.at[7 + c])

        @pl.when(origin != h)
        def _():
            away.start()

        @pl.when(origin == h)
        def _():
            here.start()

        last.append((origin, away, here))

    d_copies, last = {}, []
    order = list(range(1, chunks + 1)) + [0]
    for c in order:
        if c:
            cols = slice((c - 1) * width, c * width)
            sums = jnp.dot(
                joined, ws_all[:, :, cols].reshape(-1, width), preferred_element_type=jnp.float32
            ) + jnp.dot(
                crossed, wc_all[:, :, cols].reshape(-1, width), preferred_element_type=jnp.float32
            )
            sum_v[:, cols] = sums.astype(jnp.bfloat16)
        else:
            settle_weights(2)
            sums = jnp.dot(
                audio_joined, wa_all[...].reshape(-1, audio_width),
                preferred_element_type=jnp.float32,
            )
            sum_a[...] = sums.astype(jnp.bfloat16)
        first_hop(c)
        second_hop(c, 0)
    for c in order:
        for d in range(1, n):
            d_copies[c, d].wait_recv()
            second_hop(c, d)

    for origin, away, here in last:
        @pl.when(origin != h)
        def _():
            away.wait_send()

        @pl.when(origin == h)
        def _():
            here.wait()

    for c in order:
        out = out_a if c == 0 else out_v
        for d in range(1, n):
            who = lax.rem(h + d, n)
            target = rows_of(out, c, who)
            remote(
                target, target, e_send.at[c, 0], e_recv.at[c, n - d],
                {"wide": w, "heads": who},
            ).wait_recv()

    for copy in (
        list(a_copies.values()) + sum(w_copies, []) + sum(f_copies, [])
        + list(x_copies.values()) + list(d_copies.values())
    ):
        copy.wait_send()
    for step in range(steps):
        for way in (1, -1):
            @pl.when(sends(step, way))
            def _():
                for kind in range(2):
                    for d in range(n):
                        along(kind, d, step, way).wait_send()


def shards(*args):
    n = lax.axis_size("wide")
    count = lax.axis_size("heads")
    head_count = args[2].shape[1] // HDV
    if not (n == count == head_count and n % 2 == 0 and args[5].shape[0] % (16 * n) == 0):
        return general_shards(*args)
    (video_hidden, audio_hidden, vq, vk, vv, aq, ak, av, cvq, cak, cav, caq, cvk, cvv,
     vso, vco, aso, aco, table) = args
    rows, few = vq.shape[0], aq.shape[0]
    depth = rows + rows // 2 + 3 * few
    vmem = pl.BlockSpec(memory_space=pltpu.VMEM)
    anywhere = pl.BlockSpec(memory_space=pl.ANY)
    bf16 = jnp.bfloat16
    pack, wa, bias_v, bias_a = pl.pallas_call(
        functools.partial(pack_kernel, n),
        out_shape=(
            jax.ShapeDtypeStruct((n, depth, 2 * HDA), bf16),
            jax.ShapeDtypeStruct((2 * aso.shape[0], aso.shape[1]), bf16),
            jax.ShapeDtypeStruct((n, n * few), jnp.float32),
            jax.ShapeDtypeStruct((n, n * rows), jnp.float32),
        ),
        in_specs=[vmem] * 11 + [pl.BlockSpec(memory_space=pltpu.SMEM)],
        out_specs=(vmem, vmem, vmem, vmem),
        name="pack",
    )(cvq, cvk, cvv, aq, ak, av, caq, cak, cav, aso, aco, table)
    chunks = max(1, vso.shape[1] // 512)
    rest = rows // 2 + few
    dma = pltpu.SemaphoreType.DMA
    video_sum, audio_sum = pl.pallas_call(
        functools.partial(fused_kernel, n, chunks),
        out_shape=(
            jax.ShapeDtypeStruct(video_hidden.shape, bf16),
            jax.ShapeDtypeStruct(audio_hidden.shape, bf16),
        ),
        in_specs=[anywhere] * 7 + [vmem] * 2,
        out_specs=(anywhere, anywhere),
        scratch_shapes=[
            pltpu.VMEM((n, rows, HDV), bf16),
            pltpu.VMEM((n, rows, HDV), bf16),
            pltpu.VMEM((n, rows, HDV), bf16),
            pltpu.VMEM((n, depth, 2 * HDA), bf16),
            pltpu.VMEM((n,) + vso.shape, bf16),
            pltpu.VMEM((n,) + vco.shape, bf16),
            pltpu.VMEM((n,) + wa.shape, bf16),
            pltpu.VMEM((n, rows, HDV), bf16),
            pltpu.VMEM((n, rest, 2 * HDA), bf16),
            pltpu.VMEM((n * n, rows, HDV), bf16),
            pltpu.VMEM((n * n, rest, 2 * HDA), bf16),
            pltpu.VMEM(video_hidden.shape, bf16),
            pltpu.VMEM(audio_hidden.shape, bf16),
            pltpu.VMEM((n, rows // n, video_hidden.shape[1]), bf16),
            pltpu.VMEM((n, few // n, audio_hidden.shape[1]), bf16),
            dma((4, n)), dma((4, n)),
            dma((3, n)), dma((3, n)),
            dma((3, n)), dma((3, n)),
            dma((2, n)), dma((2, n)),
            dma((4 * n * (n - 1),)), dma((4 * n * (n - 1),)),
            dma((1 + chunks, n)), dma((1 + chunks, n)),
            dma((1 + chunks, n)), dma((1 + chunks, n)),
            dma((8 + chunks,)),
        ],
        compiler_params=pltpu.CompilerParams(collective_id=0, has_side_effects=True),
        name="joint",
    )(vq, vk, vv, pack, vso, vco, wa, bias_v, bias_a)
    video_out = video_hidden.astype(jnp.float32) + video_sum.astype(jnp.float32)
    audio_out = audio_hidden.astype(jnp.float32) + audio_sum.astype(jnp.float32)
    return (video_out.astype(bf16), audio_out.astype(bf16))


def solution(mesh):
    placed = (
        P(("groups", "wide"), "heads"),
        P(("groups", "wide"), "heads"),
        P(("groups", "wide"), "heads"),
        P(("groups", "wide"), "heads"),
        P(("groups", "wide"), "heads"),
        P(("groups", "wide"), "heads"),
        P(("groups", "wide"), "heads"),
        P(("groups", "wide"), "heads"),
        P(("groups", "wide"), "heads"),
        P(("groups", "wide"), "heads"),
        P(("groups", "wide"), "heads"),
        P(("groups", "wide"), "heads"),
        P(("groups", "wide"), "heads"),
        P(("groups", "wide"), "heads"),
        P("heads", "wide"),
        P("heads", "wide"),
        P("heads", "wide"),
        P("heads", "wide"),
        P("groups", None),
    )
    return jax.shard_map(
        shards,
        mesh=mesh,
        in_specs=placed,
        out_specs=(P(("groups", "wide"), "heads"), P(("groups", "wide"), "heads")),
        check_vma=False,
    )
```
